32 devices in a mesh: strips: 2 (over y), wave: 4 (over x, core), cols: 4 (over z).
Axes of the slice: x: 2, y: 2, z: 4, core: 2. Of those that a mesh axis runs over, the one named last changes fastest.
Arguments:
- frames: bfloat16 [1024, 32, 4096], P('wave', 'strips', 'cols'), parts along dimension 1, may hold values from -6 to 6
- wavenumbers: float32 [1024], replicated, may hold values from 0 to 1
- band_start: int32 [6], replicated, may hold values from 0 to 384
- aperture_offset: int32 [64], P(('strips', 'cols')), parts along dimension 0, may hold values from 0 to 15
- aperture_count: int32 [64], P(('strips', 'cols')), parts along dimension 0, may hold values from 4 to 16
- reference_pixels: int32 [512], P('strips'), parts along dimension 0, may hold values from 0 to 65535, as said below
Outputs:
- cavity_maps: bfloat16 [6, 2, 128, 32, 4096], P(None, None, None, ('strips', 'wave'), 'cols'), parts along dimension 3
The draws below stay inside these ranges and needn't reach their ends.
There are 2 independent parts, one for each index of `strips`. The reference program is written for one: setup_inputs(seed, part) draws one part's arguments, and reference() takes and returns one part's arrays. A program takes and returns all parts, laid end to end along the dimension named above; an argument that names none is the same for every part. Nothing has to cross between parts.
Inputs may be any that keep to these rules, and one draw needn't show every extreme that they name: `reference_pixels`: the indices are distinct.
All inputs are finite; a program needn't handle non-finite values.
Results may differ from the reference program's by a relative error of at most 0.0056.
Values may be sent and summed in bfloat16 or wider, within the bound.
No kernel may reach another device: no remote copies, remote signals or barrier semaphores. Data moves between devices by JAX's collectives and lax.ppermute only.
A program may use at most 128 MiB of HBM per device.

```python
import math
import jax
import jax.numpy as jnp
from jax import lax

F = 1024
ROWS = 16
COLBLK = 128
CAV = 6
NB = 128
REFN = 256
W = 4096
NCB = 32


def draw_reference_pixels(key, part):
    return jax.random.permutation(key, ROWS * W)[:REFN].astype(jnp.int32)


def set_ends(array, stream_key, least, top_value):
    index_at = [jax.random.randint(jax.random.fold_in(stream_key, axis), (), 0, length) for axis, length in enumerate(array.shape)]
    main_axis = array.shape.index(max(array.shape))
    neighbour = index_at[:main_axis] + [(index_at[main_axis] + 1) % array.shape[main_axis]] + index_at[main_axis + 1:]
    return array.at[tuple(index_at)].set(least).at[tuple(neighbour)].set(top_value)


def level_of(own_key, extent, shards, low, largest):
    def one(position, shards_of):
        draws = jax.random.uniform(jax.random.fold_in(jax.random.fold_in(own_key, 6), position), (shards_of,), jnp.float32, low / len(shards), largest / len(shards))
        return jnp.repeat(jnp.exp(draws), extent[position] // shards_of).reshape((-1,) + (1,) * (len(extent) - position - 1))

    level = one(*shards[0])
    for cut in shards[1:]:
        level = level * one(*cut)
    return level


def scatter_about(stream_key, dims, spread, most, shards=(), kind=jnp.bfloat16):
    result = jax.random.normal(stream_key, dims, jnp.float32) * spread
    if len(shards) > 0:
        result = level_of(stream_key, dims, shards, -0.22, 0.18) * result
    return jnp.clip(result, min=-most, max=most).astype(kind)


def setup_inputs(seed: int = 0, part: int = 0) -> dict:
    key_list = jax.random.split(jax.random.key(seed), 7)
    part_splits = jax.random.split(jax.random.fold_in(key_list[6], part), 7)
    return {
        "frames": scatter_about(part_splits[0], (F, ROWS, W), 1.0, 6.0, ((0, 4), (2, 4))),
        "wavenumbers": jnp.clip(jax.random.uniform(key_list[1], (F,), jnp.float32, 0.0, 1.0), 0.0, 1.0),
        "band_start": set_ends(jax.random.randint(key_list[2], (CAV,), 0, F // 2 - NB + 1), jax.random.fold_in(key_list[2], 1), 0, (F // 2 - NB + 1) - 1).astype(jnp.int32),
        "aperture_offset": set_ends(jax.random.randint(part_splits[3], (NCB,), 0, ROWS), jax.random.fold_in(part_splits[3], 1), 0, ROWS - 1).astype(jnp.int32),
        "aperture_count": set_ends(jax.random.randint(part_splits[4], (NCB,), 4, ROWS + 1), jax.random.fold_in(part_splits[4], 1), 4, ROWS).astype(jnp.int32),
        "reference_pixels": draw_reference_pixels(jax.random.fold_in(jax.random.fold_in(key_list[6], part), 71), part),
    }


TWO_PI = 2.0 * math.pi
EPS = 1e-06

def table_block(wavenumbers, band_start, first_row, count, bins_band, frame_total):
    rows = first_row + jnp.arange(count, dtype=jnp.int32)
    cavity = rows // (2 * bins_band)
    imag_part = rows // bins_band % 2
    offset_bin = rows % bins_band
    cav_ids = jnp.arange(band_start.shape[0], dtype=jnp.int32)
    start_of = lax.optimization_barrier(jnp.sum(jnp.where(cavity[:, None] == cav_ids[None, :], band_start[None, :], 0), axis=1))
    bins = (start_of + offset_bin).astype(jnp.float32)
    frame_pos = jnp.arange(frame_total, dtype=jnp.float32)
    window = (0.5 - 0.5 * jnp.cos(TWO_PI * (frame_pos + 0.5) / frame_total)) / math.sqrt(frame_total)
    angle_mat = bins[:, None] * wavenumbers[None, :] * TWO_PI
    value = jnp.where(imag_part[:, None] == 0, jnp.cos(angle_mat), -jnp.sin(angle_mat)) * window[None, :]
    return value.astype(jnp.bfloat16)

def reference(frames, wavenumbers, band_start, aperture_offset, aperture_count, reference_pixels):
    blocks = lax.map(lambda c: table_block(wavenumbers, band_start, c * 2 * NB, 2 * NB, NB, F), jnp.arange(CAV, dtype=jnp.int32))
    table = blocks.reshape(2 * CAV * NB, F)
    col_block = jnp.arange(W, dtype=jnp.int32) // COLBLK
    off_cols = aperture_offset[col_block]
    cnt_cols = aperture_count[col_block]
    row_ids = jnp.arange(ROWS, dtype=jnp.int32)[:, None]
    valid = ((row_ids >= off_cols[None, :]) & (row_ids < off_cols[None, :] + cnt_cols[None, :])).astype(jnp.bfloat16)
    flat_frames = frames.reshape(F, ROWS * W)
    flat_valid = valid.reshape(ROWS * W)
    ref_frames = flat_frames[:, reference_pixels] * flat_valid[reference_pixels][None, :]
    ref_spec = jnp.dot(table, ref_frames, preferred_element_type=jnp.float32).reshape(CAV, 2, NB, REFN)
    middle = ref_spec[:, :, NB // 2, :]
    ref_re = lax.optimization_barrier(jnp.sum(middle[:, 0], axis=1))
    ref_im = lax.optimization_barrier(jnp.sum(middle[:, 1], axis=1))
    power = lax.optimization_barrier(jnp.sum(middle[:, 0] * middle[:, 0] + middle[:, 1] * middle[:, 1], axis=1))
    scale = 1.0 / jnp.sqrt(power + EPS)

    def one_row(row):
        row_frames = lax.dynamic_index_in_dim(frames, row, 1, keepdims=False)
        row_valid = lax.dynamic_index_in_dim(valid, row, 0, keepdims=False)
        spec = jnp.dot(table, row_frames * row_valid[None, :], preferred_element_type=jnp.float32).reshape(CAV, 2, NB, W)
        real_part = spec[:, 0]
        imag_part = spec[:, 1]
        out_re = (real_part * ref_re[:, None, None] + imag_part * ref_im[:, None, None]) * scale[:, None, None]
        out_im = (imag_part * ref_re[:, None, None] - real_part * ref_im[:, None, None]) * scale[:, None, None]
        return jnp.stack([out_re, out_im], axis=1).astype(jnp.bfloat16)
    rows_out = lax.map(one_row, jnp.arange(ROWS, dtype=jnp.int32))
    return jnp.transpose(rows_out, (1, 2, 3, 0, 4))
```

```python
import functools
import math

import jax
import jax.numpy as jnp
from jax import lax
from jax.experimental import pallas as pl
from jax.experimental.pallas import tpu as pltpu
from jax.sharding import PartitionSpec as P

NB = 128
LANES = 128
EPS = 1e-06
QP = 16


def params(**kw):
    return pltpu.CompilerParams(vmem_limit_bytes=48 * 2**20, **kw)


def chunk_plan(cols):
    unit = cols // 8
    if unit % LANES:
        return [(0, cols)]
    return [(7, unit), (0, 2 * unit), (1, 2 * unit), (2, 2 * unit), (6, unit)]


def prep_kernel(nw, rows, block_cols, first_col, wid, off, cnt, x_ref, *outs):
    fd, rows_all, width = x_ref.shape
    group = 256 // rows_all
    me = wid[0]
    i = lax.broadcasted_iota(jnp.int32, (256, 256), 0)
    j = lax.broadcasted_iota(jnp.int32, (256, 256), 1)
    slot = i // group
    row = ((slot // rows) ^ me) * rows + slot % rows
    pick = ((j // rows_all == i % group) & (j % rows_all == row)).astype(jnp.bfloat16)
    keep = []
    for s in range(rows_all):
        r = ((s // rows) ^ me) * rows + s % rows
        per_block = []
        for b in range(width // block_cols):
            lo = off[first_col // block_cols + b]
            inside = (r >= lo) & (r < lo + cnt[first_col // block_cols + b])
            per_block.append(jnp.where(inside, 1.0, 0.0))
        keep.append(per_block)
    for g in range(fd // group):
        xg = x_ref[group * g : group * (g + 1)].reshape(256, width)
        y = jnp.dot(pick, xg, preferred_element_type=jnp.float32)
        for s in range(rows_all):
            part = y[s * group : (s + 1) * group]
            part = jnp.concatenate(
                [
                    part[:, b * block_cols : (b + 1) * block_cols] * keep[s][b]
                    for b in range(width // block_cols)
                ],
                axis=1,
            )
            outs[s // rows][s % rows, group * g : group * (g + 1), :] = part.astype(jnp.bfloat16)


def prep(frames, wid, off, cnt, nw, block, width):
    fd, rows_all, cols = frames.shape
    rows = rows_all // nw
    block_cols = cols // off.shape[0]
    return pl.pallas_call(
        functools.partial(prep_kernel, nw, rows, block_cols, block * width),
        grid_spec=pltpu.PrefetchScalarGridSpec(
            num_scalar_prefetch=3,
            grid=(1,),
            in_specs=[pl.BlockSpec((fd, rows_all, width), lambda g, *_: (0, 0, block))],
            out_specs=[pl.BlockSpec((rows, fd, width), lambda g, *_: (0, 0, 0))] * nw,
        ),
        out_shape=[jax.ShapeDtypeStruct((rows, fd, width), jnp.bfloat16)] * nw,
        compiler_params=params(),
        cost_estimate=pl.CostEstimate(
            flops=2 * 256 * fd * rows_all * width,
            bytes_accessed=4 * fd * rows_all * width,
            transcendentals=0,
        ),
        name=f"prep{block}",
    )(wid, off, cnt, frames)


def cos_sin_turns(turns):
    quarters = turns * 4.0
    near = jnp.floor(quarters + 0.5)
    x = (quarters - near) * (math.pi / 2)
    z = x * x
    s = x * (
        1.0
        + z
        * (-1.0 / 6 + z * (1.0 / 120 + z * (-1.0 / 5040 + z * (1.0 / 362880))))
    )
    c = 1.0 + z * (
        -0.5 + z * (1.0 / 24 + z * (-1.0 / 720 + z * (1.0 / 40320 + z * (-1.0 / 3628800))))
    )
    q = near.astype(jnp.int32) & 3
    odd = (q & 1) == 1
    cos = jnp.where(odd, s, c)
    sin = jnp.where(odd, c, s)
    cos = jnp.where((q == 1) | (q == 2), -cos, cos)
    sin = jnp.where(q >= 2, -sin, sin)
    return cos, sin


def table_kernel(frame_total, start, wn_ref, pos_ref, t_ref):
    nb = t_ref.shape[0] // 2
    window = (
        0.5 - 0.5 * jnp.cos((2.0 * math.pi) * (pos_ref[...] + 0.5) / frame_total)
    ) / math.sqrt(frame_total)
    first = start[pl.program_id(0)]
    for h in range(0, nb, 16):
        bins = (first + h + lax.broadcasted_iota(jnp.int32, (16, 1), 0)).astype(jnp.float32)
        phase = bins * wn_ref[...]
        cos, sin = cos_sin_turns(phase - jnp.floor(phase))
        t_ref[h : h + 16, :] = (cos * window).astype(jnp.bfloat16)
        t_ref[nb + h : nb + h + 16, :] = (-sin * window).astype(jnp.bfloat16)


def make_table(band_start, wn, pos):
    frame_total = wn.shape[1]
    ncav = band_start.shape[0]
    return pl.pallas_call(
        functools.partial(table_kernel, frame_total),
        grid_spec=pltpu.PrefetchScalarGridSpec(
            num_scalar_prefetch=1,
            grid=(ncav,),
            in_specs=[pl.BlockSpec((1, frame_total), lambda c, _: (0, 0))] * 2,
            out_specs=pl.BlockSpec((2 * NB, frame_total), lambda c, _: (c, 0)),
        ),
        out_shape=jax.ShapeDtypeStruct((ncav * 2 * NB, frame_total), jnp.bfloat16),
        compiler_params=params(),
        cost_estimate=pl.CostEstimate(
            flops=60 * ncav * NB * frame_total,
            bytes_accessed=4 * ncav * NB * frame_total,
            transcendentals=0,
        ),
        name="table",
    )(band_start, wn, pos)


def reference_kernel(nw, plan, base_col, wid, tm_ref, col_ref, row_ref, *rest):
    pieces = rest[:-2]
    o_ref, mid = rest[-2:]
    step = pl.program_id(0)
    rows = pl.num_programs(0)
    for i, (block, width) in enumerate(plan):
        for k in range(nw):
            part = jnp.dot(tm_ref[...], pieces[i * nw + k][0], preferred_element_type=jnp.float32)
            mid[k, :, block * width : (block + 1) * width] = part

    @pl.when(step == 0)
    def _():
        o_ref[...] = jnp.zeros_like(o_ref)

    cols = mid.shape[2]
    npix = col_ref.shape[1]
    x = lax.broadcasted_iota(jnp.int32, (cols, npix), 0) + base_col[0]
    hot = (x == col_ref[...]).astype(jnp.bfloat16)
    left = mid[...].reshape(nw * QP, cols)
    total = jnp.zeros((nw * QP, npix), jnp.float32)
    for _ in range(3):
        high = left.astype(jnp.bfloat16)
        total = total + jnp.dot(high, hot, preferred_element_type=jnp.float32)
        left = left - high.astype(jnp.float32)
    acc = o_ref[...]
    for k in range(nw):
        here = row_ref[...] == ((wid[0] ^ k) * rows + step)
        acc = acc + jnp.where(here, total[k * QP : (k + 1) * QP], 0.0)
    o_ref[...] = acc


def reference_part(pieces, tm, wid, base_col, col, row, nw, plan, cols):
    rows, fd, _ = pieces[0].shape
    npix = col.shape[1]
    specs = []
    for _, width in plan:
        specs += [pl.BlockSpec((1, fd, width), lambda r, *_: (r, 0, 0))] * nw
    return pl.pallas_call(
        functools.partial(reference_kernel, nw, plan),
        grid_spec=pltpu.PrefetchScalarGridSpec(
            num_scalar_prefetch=2,
            grid=(rows,),
            in_specs=[
                pl.BlockSpec((QP, fd), lambda r, *_: (0, 0)),
                pl.BlockSpec((1, npix), lambda r, *_: (0, 0)),
                pl.BlockSpec((1, npix), lambda r, *_: (0, 0)),
            ]
            + specs,
            out_specs=pl.BlockSpec((QP, npix), lambda r, *_: (0, 0)),
            scratch_shapes=[pltpu.VMEM((nw, QP, cols), jnp.float32)],
        ),
        out_shape=jax.ShapeDtypeStruct((QP, npix), jnp.float32),
        compiler_params=params(),
        cost_estimate=pl.CostEstimate(
            flops=2 * QP * fd * rows * nw * cols * 3,
            bytes_accessed=2 * fd * rows * nw * cols,
            transcendentals=0,
        ),
        name="reference_part",
    )(base_col, wid, tm, col, row, *pieces)


def main_kernel(nw, sc, t_ref, *rest):
    xs = rest[:nw]
    o_ref, xc, ys = rest[-3:]
    step = pl.program_id(0)
    rows, fd, width = xs[0].shape
    ncav = o_ref.shape[0]

    @pl.when(step == 0)
    def _():
        for k in range(nw):
            for r in range(rows):
                xc[k * fd : (k + 1) * fd, r * width : (r + 1) * width] = xs[k][r]

    ys[...] = jnp.dot(t_ref[...], xc[...], preferred_element_type=jnp.float32)
    nbin = min(NB, 256 // rows)
    size = nbin * rows
    i = lax.broadcasted_iota(jnp.int32, (size, size), 0)
    j = lax.broadcasted_iota(jnp.int32, (size, size), 1)
    mix = ((j % nbin == i // rows) & (j // nbin == i % rows)).astype(jnp.bfloat16)
    for c in range(ncav):
        a = sc[step * ncav + c, 0]
        b = sc[step * ncav + c, 1]
        for h in range(NB // nbin):
            re = ys[2 * c * NB + h * nbin : 2 * c * NB + (h + 1) * nbin, :]
            im = ys[(2 * c + 1) * NB + h * nbin : (2 * c + 1) * NB + (h + 1) * nbin, :]
            for q, v in enumerate((re * a + im * b, im * a - re * b)):
                v = v.astype(jnp.bfloat16)
                if rows > 1:
                    v = jnp.concatenate(
                        [v[:, r * width : (r + 1) * width] for r in range(rows)], axis=0
                    )
                    v = jnp.dot(mix, v, preferred_element_type=jnp.float32).astype(jnp.bfloat16)
                o_ref[c, q, h * nbin : (h + 1) * nbin] = v.reshape(nbin, rows, width)


def transform(sc, table, xs, prev, nw, block, cols, per_step):
    rows, fd, width = xs[0].shape
    ncav = sc.shape[0]
    frame_total = table.shape[1]
    operands = [sc, table, *xs]
    specs = [pl.BlockSpec((2 * NB * per_step, frame_total), lambda c, _: (c, 0))]
    specs += [pl.BlockSpec((rows, fd, width), lambda c, _: (0, 0, 0))] * nw
    alias = {}
    if prev is not None:
        alias = {len(operands): 0}
        operands.append(prev)
        specs.append(pl.BlockSpec(memory_space=pl.ANY))
    return pl.pallas_call(
        functools.partial(main_kernel, nw),
        grid_spec=pltpu.PrefetchScalarGridSpec(
            num_scalar_prefetch=1,
            grid=(ncav // per_step,),
            in_specs=specs,
            out_specs=pl.BlockSpec((per_step, 2, NB, rows, width), lambda c, _: (c, 0, 0, 0, block)),
            scratch_shapes=[
                pltpu.VMEM((frame_total, rows * width), jnp.bfloat16),
                pltpu.VMEM((2 * NB * per_step, rows * width), jnp.float32),
            ],
        ),
        out_shape=jax.ShapeDtypeStruct((ncav, 2, NB, rows, cols), jnp.bfloat16),
        input_output_aliases=alias,
        compiler_params=params(),
        cost_estimate=pl.CostEstimate(
            flops=2 * ncav * 2 * NB * frame_total * rows * width,
            bytes_accessed=2 * ncav * 2 * NB * (frame_total + rows * width),
            transcendentals=0,
        ),
        name=f"transform{block}",
    )(*operands)


def shards(frames, wavenumbers, band_start, aperture_offset, aperture_count, reference_pixels):
    fd, rows_all, cols = frames.shape
    frame_total = wavenumbers.shape[0]
    ncav = band_start.shape[0]
    nw = lax.axis_size("wave")
    nc = lax.axis_size("cols")
    rows = rows_all // nw
    me = lax.axis_index("wave")
    wid = me.astype(jnp.int32).reshape(1)
    plan = chunk_plan(cols)

    def exchange(pieces):
        return [pieces[0]] + [
            lax.ppermute(pieces[k], "wave", [(i, i ^ k) for i in range(nw)])
            for k in range(1, nw)
        ]

    sent = [prep(frames, wid, aperture_offset, aperture_count, nw, b, w) for b, w in plan]
    got = [exchange(p) for p in sent]

    order = me ^ jnp.arange(nw, dtype=jnp.int32)
    wn = wavenumbers.reshape(nw, fd)[order].reshape(1, frame_total)
    pos = (order[:, None] * fd + jnp.arange(fd, dtype=jnp.int32)[None, :]).astype(jnp.float32)
    table = make_table(band_start, wn, pos.reshape(1, frame_total))

    tm = table.reshape(2 * ncav, NB, frame_total)[:, NB // 2, :fd]
    tm = jnp.pad(tm, ((0, QP - 2 * ncav), (0, 0)))
    width_all = cols * nc
    row = (reference_pixels // width_all)[None, :]
    col = (reference_pixels % width_all)[None, :]
    base_col = (lax.axis_index("cols") * cols).astype(jnp.int32).reshape(1)
    flat = [x for p in sent for x in p]
    part = reference_part(flat, tm, wid, base_col, col, row, nw, plan, cols)
    middle = part
    for k in range(1, nw):
        middle = middle + lax.ppermute(part, "wave", [(i, i ^ k) for i in range(nw)])
    middle = middle[: 2 * ncav].reshape(ncav, 2, -1)
    re, im = middle[:, 0], middle[:, 1]
    mine = jnp.stack(
        [jnp.sum(re, axis=1), jnp.sum(im, axis=1), jnp.sum(re * re + im * im, axis=1)]
    )
    sums = mine
    for k in range(1, nc):
        sums = sums + lax.ppermute(mine, "cols", [(i, (i + k) % nc) for i in range(nc)])
    scale = 1.0 / jnp.sqrt(sums[2] + EPS)
    sc = jnp.stack([sums[0] * scale, sums[1] * scale], axis=1)

    out = None
    for (block, _), xs in zip(plan, got):
        out = transform(sc, table, xs, out, nw, block, cols, 2)
    return out


def solution(mesh):
    placed = (
        P("wave", "strips", "cols"),
        P(),
        P(),
        P(("strips", "cols")),
        P(("strips", "cols")),
        P("strips"),
    )
    return jax.shard_map(
        shards,
        mesh=mesh,
        in_specs=placed,
        out_specs=P(None, None, None, ("strips", "wave"), "cols"),
        check_vma=False,
    )
```
